32 devices in a mesh: dp: 4 (over z), rep: 2 (over y), grp: 4 (over x, core).
Axes of the slice: x: 2, y: 2, z: 4, core: 2. Of those that a mesh axis runs over, the one named last changes fastest.
Arguments:
- grad_parts: float32 [8, 8, 192, 2048], P(('rep', 'grp'), None, 'dp'), may hold values from -6 to 6
- momentum: float32 [8, 192, 2048], P(None, 'dp', ('rep', 'grp')), may hold values from -24 to 24
- layer_live: int32 [8], replicated, may hold values from 0 to 1, as said below
Outputs:
- new_momentum: float32 [8, 192, 2048], P(None, 'dp', ('rep', 'grp'))
- orth_update: bfloat16 [8, 192, 2048], P(None, 'dp', ('rep', 'grp'))
The draws below stay inside these ranges and needn't reach their ends.
Inputs may be any that keep to these rules, and one draw needn't show every extreme that they name: `layer_live`: at least one matrix is live in every draw.
All inputs are finite; a program needn't handle non-finite values.
Results may differ from the reference program's by a relative error of at most 0.028.
Values may be sent and summed in bfloat16 or wider, within the bound.
A program may use at most 64 MiB of HBM per device.

```python
import math
import jax
import jax.numpy as jnp
from jax import lax

ROWS = 192
C = 2048
ITERS = 5
MATS = 8
REPLICAS = 8


def draw_layer_live(key, part):
    first_key, second_key = jax.random.split(jax.random.fold_in(key, 17))
    coin_flips = jax.random.randint(first_key, (MATS,), 0, 2, dtype=jnp.int32)
    chosen = jax.random.randint(second_key, (), 0, MATS, dtype=jnp.int32)
    forced = (jnp.arange(MATS, dtype=jnp.int32) == chosen).astype(jnp.int32)
    return jnp.maximum(coin_flips, forced)


def spiked(array, own_key, source, target, shards_of, factor):
    owner, partner = [(jnp.arange(array.shape[axis_at]) // (array.shape[axis_at] // shards_of)).reshape([-1 if axis == axis_at else 1 for axis in range(array.ndim)]) for axis_at in (source, target)]
    chosen = jax.random.permutation(own_key, shards_of)[partner]
    strong = (owner == chosen) | (owner == (partner + shards_of // 2) % shards_of)
    return jnp.where(strong, factor * array, array)


def block_levels(own_key, shape, pieces, least, largest):
    gain = 1.0
    for axis_at, shards_of in pieces:
        draws = jax.random.uniform(jax.random.fold_in(jax.random.fold_in(own_key, 6), axis_at), (shards_of,), jnp.float32, least / len(pieces), largest / len(pieces))
        gain = gain * jnp.repeat(jnp.exp(draws), shape[axis_at] // shards_of).reshape((-1,) + (1,) * (len(shape) - 1 - axis_at))
    return gain


def bell_draw(stream_key, shape, spread, most, shards=(), held_as=jnp.bfloat16):
    drawn = spread * jax.random.normal(stream_key, shape, jnp.float32)
    if shards:
        drawn = drawn * block_levels(stream_key, shape, shards, -0.22, 0.18)
    return jnp.clip(drawn, -most, most).astype(held_as)


def heavy_noise(key, shape, deviation, limit, cuts, heavy, kind=jnp.bfloat16):
    result = deviation * jax.random.normal(key, shape, jnp.float32)
    if cuts:
        result = result * block_levels(key, shape, cuts, -0.22, 0.18)
    return jnp.clip(spiked(result, jax.random.fold_in(key, 3), *heavy), -limit, limit).astype(kind)


def setup_inputs(seed: int = 0) -> dict:
    seeds = jax.random.split(jax.random.key(seed), 4)
    grad_parts = heavy_noise(seeds[0], (REPLICAS, MATS, ROWS, C), 1.0, 6.0, ((0, 8), (2, 4)), (0, 3, 8, 2.0), jnp.float32)
    momentum = bell_draw(seeds[1], (MATS, ROWS, C), 4.0, 24.0, ((1, 4), (2, 8)), jnp.float32)
    layer_live = draw_layer_live(jax.random.fold_in(seeds[3], 71), 0)
    return dict(grad_parts=grad_parts, momentum=momentum, layer_live=layer_live)


decay_rate = 0.95
first_coef = 3.4445
second_coef = -4.775
third_coef = 2.0315
norm_eps = 1e-07

def newton_schulz(source):
    source_f32 = source.astype(jnp.float32)
    frob_norm = jnp.sqrt(jnp.sum(source_f32 * source_f32))
    current = (source_f32 / (frob_norm + norm_eps)).astype(jnp.bfloat16)
    next_iterate = source_f32
    for iteration in range(ITERS):
        gram_matrix = lax.dot_general(current, current, (((1,), (1,)), ((), ())), preferred_element_type=jnp.float32).astype(jnp.bfloat16)
        squared = jnp.dot(gram_matrix, gram_matrix, preferred_element_type=jnp.float32)
        polynomial = (second_coef * gram_matrix.astype(jnp.float32) + third_coef * squared).astype(jnp.bfloat16)
        next_iterate = first_coef * current.astype(jnp.float32) + jnp.dot(polynomial, current, preferred_element_type=jnp.float32)
        if iteration + 1 < ITERS:
            current = next_iterate.astype(jnp.bfloat16)
    return (next_iterate * math.sqrt(source.shape[1])).astype(jnp.bfloat16)

def reference(grad_parts, momentum, layer_live):
    grad_sum = lax.optimization_barrier(jnp.sum(grad_parts, axis=0))
    active = (layer_live > 0)[:, None, None]
    new_momentum = jnp.where(active, decay_rate * momentum + grad_sum, momentum)
    sources = new_momentum.astype(jnp.bfloat16)
    updates = lax.map(newton_schulz, sources)
    orth_update = jnp.where(active, updates, jnp.zeros_like(updates))
    return (new_momentum, orth_update)
```

```python
import functools
import math

import jax
import jax.numpy as jnp
from jax import lax
from jax.experimental import pallas as pl
from jax.experimental.pallas import tpu as pltpu
from jax.sharding import PartitionSpec as P

ITERS = 5


decay_rate = 0.95
first_coef = 3.4445
second_coef = -4.775
third_coef = 2.0315
norm_eps = 1e-07


def newton_schulz(source):
    source_f32 = source.astype(jnp.float32)
    frob_norm = jnp.sqrt(jnp.sum(source_f32 * source_f32))
    current = (source_f32 / (frob_norm + norm_eps)).astype(jnp.bfloat16)
    next_iterate = source_f32
    for iteration in range(ITERS):
        gram_matrix = lax.dot_general(
            current, current, (((1,), (1,)), ((), ())), preferred_element_type=jnp.float32
        ).astype(jnp.bfloat16)
        squared = jnp.dot(gram_matrix, gram_matrix, preferred_element_type=jnp.float32)
        polynomial = (second_coef * gram_matrix.astype(jnp.float32) + third_coef * squared).astype(
            jnp.bfloat16
        )
        next_iterate = first_coef * current.astype(jnp.float32) + jnp.dot(
            polynomial, current, preferred_element_type=jnp.float32
        )
        if iteration + 1 < ITERS:
            current = next_iterate.astype(jnp.bfloat16)
    return (next_iterate * math.sqrt(source.shape[1])).astype(jnp.bfloat16)


def zero_result(matrix):
    return jnp.zeros_like(matrix)


def guarded(matrix):
    return lax.cond(jnp.any(matrix != 0), newton_schulz, zero_result, matrix)


def per_device(grad_parts, momentum, layer_live):
    width = momentum.shape[2]
    col_start = lax.axis_index(("rep", "grp")) * width
    active = (layer_live > 0)[:, None, None]
    summed_share = lax.psum_scatter(grad_parts[0], ("rep", "grp"), scatter_dimension=2, tiled=True)
    fresh_momentum = jnp.where(active, decay_rate * momentum + summed_share, momentum)
    sources = lax.all_gather(
        fresh_momentum.astype(jnp.bfloat16), ("rep", "grp"), axis=2, tiled=True
    )
    owners = lax.axis_size("dp")
    matrices = layer_live.shape[0]
    per_owner = matrices // owners
    piece_rows = sources.shape[1]
    col_count = sources.shape[2]
    matrix_ids = jnp.arange(matrices, dtype=jnp.int32)
    live_flag = (layer_live > 0).astype(jnp.int32)
    slot_pos = matrix_ids % per_owner * owners + matrix_ids // per_owner
    slot_ids = jnp.arange(matrices, dtype=jnp.int32)
    placing = slot_pos[None, :] == slot_ids[:, None]
    holder = jnp.sum(jnp.where(placing, matrix_ids[None, :], 0), axis=1)
    filled = jnp.sum(placing.astype(jnp.int32) * live_flag[None, :], axis=1)
    picked_rows = jnp.take(sources, holder, axis=0)
    outgoing = jnp.where(filled[:, None, None] > 0, picked_rows, jnp.zeros_like(picked_rows))
    outgoing = outgoing.reshape(per_owner, owners, piece_rows, col_count)
    blocks = lax.all_to_all(outgoing, "dp", split_axis=1, concat_axis=1, tiled=True)
    item_count = blocks.shape[0]
    stacked = blocks.reshape(item_count, owners * piece_rows, col_count)
    results = lax.map(guarded, stacked)
    results = results.reshape(item_count, owners, piece_rows, col_count)
    returned = lax.all_to_all(results, "dp", split_axis=1, concat_axis=1, tiled=True)
    returned = returned.reshape(matrices, piece_rows, col_count)
    own_cols = lax.dynamic_slice_in_dim(returned, col_start, width, 2)
    gathered = jnp.take(own_cols, jnp.maximum(slot_pos, 0), axis=0)
    orth_update = jnp.where(active, gathered, jnp.zeros_like(gathered))
    return (fresh_momentum, orth_update)


MESH = pl.DeviceIdType.MESH


def f32_dot(left, right):
    return jnp.dot(
        left.astype(jnp.bfloat16), right.astype(jnp.bfloat16), preferred_element_type=jnp.float32
    )


def orthogonalizer(gram):
    rows = gram.shape[0]
    row_ids = lax.broadcasted_iota(jnp.int32, (rows, rows), 0)
    col_ids = lax.broadcasted_iota(jnp.int32, (rows, rows), 1)
    on_diag = row_ids == col_ids
    diag = jnp.where(on_diag, gram, 0.0)
    squares = jnp.sum(jnp.sum(diag, axis=1, keepdims=True), axis=0, keepdims=True)
    inverse = 1.0 / (jnp.sqrt(squares) + norm_eps)
    current = gram * inverse * inverse
    product = None
    for iteration in range(ITERS):
        squared = f32_dot(current, current)
        higher = second_coef * current + third_coef * squared
        if product is None:
            product = jnp.where(on_diag, first_coef, 0.0) + higher
        else:
            product = first_coef * product + f32_dot(higher, product)
        if iteration + 1 < ITERS:
            half = first_coef * current + f32_dot(higher, current)
            current = first_coef * half + f32_dot(higher, half)
    return product * inverse


def step_kernel(
    sizes, grad_ref, mom_ref, live_ref, new_ref, orth_ref,
    gbuf, sbuf, rbuf, zsend, xbuf, gsend, grecv, gsum, gfull, osend, orecv,
    lsem, ssem, rsem, zssem, zrsem, gssem, grsem, assem, arsem, ossem, orsem, csem,
):
    group, owners, per_group, n, rows, width = sizes
    per = n // owners
    full = owners * rows
    share = per * full // group
    me_d = lax.axis_index("dp")
    me = lax.axis_index("rep") * per_group + lax.axis_index("grp")

    def peer_index(k):
        return lax.rem(me + k, group)

    def peer_id(k):
        peer = peer_index(k)
        return {"rep": peer // per_group, "grp": lax.rem(peer, per_group)}

    def owner_index(k):
        return lax.rem(me_d + k, owners)

    loads = []
    for k in list(range(1, group)) + [0]:
        start = pl.multiple_of(peer_index(k) * width, width)
        load = pltpu.make_async_copy(
            grad_ref.at[0, :, :, pl.ds(start, width)], gbuf.at[k], lsem.at[k]
        )
        load.start()
        loads.append(load)
    barrier = pltpu.get_barrier_semaphore()
    for k in range(1, group):
        pl.semaphore_signal(barrier, inc=1, device_id=peer_id(k), device_id_type=MESH)
    for k in range(1, owners):
        pl.semaphore_signal(barrier, inc=1, device_id={"dp": owner_index(k)}, device_id_type=MESH)
    pl.semaphore_wait(barrier, group + owners - 2)

    sends = []
    for k in range(1, group):
        loads[k - 1].wait()
        sbuf[k - 1] = gbuf[k].astype(jnp.bfloat16)
        copy = pltpu.make_async_remote_copy(
            src_ref=sbuf.at[k - 1], dst_ref=rbuf.at[k - 1],
            send_sem=ssem.at[k - 1], recv_sem=rsem.at[k - 1],
            device_id=peer_id(k), device_id_type=MESH,
        )
        copy.start()
        sends.append(copy)
    loads[group - 1].wait()
    for copy in sends:
        copy.wait_recv()
    for i in range(n):
        total = gbuf[0, i]
        for k in range(1, group):
            total = total + rbuf[k - 1, i].astype(jnp.float32)
        old = mom_ref[i]
        fresh = jnp.where(live_ref[i] > 0, decay_rate * old + total, old)
        new_ref[i] = fresh
        zsend[i] = fresh.astype(jnp.bfloat16)

    my_rows = pl.ds(pl.multiple_of(me_d * rows, rows), rows)
    own = pltpu.make_async_copy(
        zsend.at[pl.ds(me_d * per, per)], xbuf.at[:, my_rows, :], csem.at[0]
    )
    own.start()
    zcopies = []
    for k in range(1, owners):
        copy = pltpu.make_async_remote_copy(
            src_ref=zsend.at[pl.ds(owner_index(k) * per, per)], dst_ref=xbuf.at[:, my_rows, :],
            send_sem=zssem.at[k - 1], recv_sem=zrsem.at[k - 1],
            device_id={"dp": owner_index(k)}, device_id_type=MESH,
        )
        copy.start()
        zcopies.append(copy)
    own.wait()
    for copy in zcopies:
        copy.wait_recv()

    for m in range(per):
        block = xbuf[m]
        gram = lax.dot_general(
            block, block, (((1,), (1,)), ((), ())), preferred_element_type=jnp.float32
        )
        gsend[m * full : (m + 1) * full] = gram.astype(jnp.bfloat16)
    gcopies = []
    for k in range(1, group):
        start = pl.multiple_of(peer_index(k) * share, share)
        copy = pltpu.make_async_remote_copy(
            src_ref=gsend.at[pl.ds(start, share)], dst_ref=grecv.at[k - 1],
            send_sem=gssem.at[k - 1], recv_sem=grsem.at[k - 1],
            device_id=peer_id(k), device_id_type=MESH,
        )
        copy.start()
        gcopies.append(copy)
    my_share = pl.ds(pl.multiple_of(me * share, share), share)
    total = gsend[my_share].astype(jnp.float32)
    for k in range(1, group):
        gcopies[k - 1].wait_recv()
        total = total + grecv[k - 1].astype(jnp.float32)
    gsum[...] = total.astype(jnp.bfloat16)
    acopies = []
    for k in range(1, group):
        copy = pltpu.make_async_remote_copy(
            src_ref=gsum, dst_ref=gfull.at[my_share],
            send_sem=assem.at[k - 1], recv_sem=arsem.at[k - 1],
            device_id=peer_id(k), device_id_type=MESH,
        )
        copy.start()
        acopies.append(copy)
    gfull[my_share] = gsum[...]
    for copy in acopies:
        copy.wait_recv()

    scale = math.sqrt(width * group)
    factors = [
        (orthogonalizer(gfull[m * full : (m + 1) * full].astype(jnp.float32)) * scale)
        for m in range(per)
    ]
    for m in range(per):
        osend[m] = f32_dot(factors[m], xbuf[m]).astype(jnp.bfloat16)
    own = pltpu.make_async_copy(
        osend.at[:, my_rows, :], orecv.at[pl.ds(me_d * per, per)], csem.at[1]
    )
    own.start()
    ocopies = []
    for k in range(1, owners):
        their_rows = pl.ds(pl.multiple_of(owner_index(k) * rows, rows), rows)
        copy = pltpu.make_async_remote_copy(
            src_ref=osend.at[:, their_rows, :], dst_ref=orecv.at[pl.ds(me_d * per, per)],
            send_sem=ossem.at[k - 1], recv_sem=orsem.at[k - 1],
            device_id={"dp": owner_index(k)}, device_id_type=MESH,
        )
        copy.start()
        ocopies.append(copy)
    for copies in (sends, zcopies, gcopies, acopies):
        for copy in copies:
            copy.wait_send()
    own.wait()
    for copy in ocopies:
        copy.wait_recv()
    for i in range(n):
        part = orecv[i]
        orth_ref[i] = jnp.where(live_ref[i] > 0, part.astype(jnp.float32), 0.0).astype(jnp.bfloat16)
    for copy in ocopies:
        copy.wait_send()


def fused_step(mesh, grad_parts, momentum, layer_live):
    n, rows, width = momentum.shape
    owners, per_group = mesh.shape["dp"], mesh.shape["grp"]
    group = mesh.shape["rep"] * per_group
    per = n // owners
    full = owners * rows
    share = per * full // group
    live = jnp.broadcast_to(layer_live.astype(jnp.float32)[:, None, None], (n, 1, width))
    bf16, f32 = jnp.bfloat16, jnp.float32
    dma = pltpu.SemaphoreType.DMA
    vmem = pl.BlockSpec(memory_space=pltpu.VMEM)
    return pl.pallas_call(
        functools.partial(step_kernel, (group, owners, per_group, n, rows, width)),
        out_shape=(
            jax.ShapeDtypeStruct((n, rows, width), f32),
            jax.ShapeDtypeStruct((n, rows, width), bf16),
        ),
        in_specs=[pl.BlockSpec(memory_space=pl.ANY), vmem, vmem],
        out_specs=(vmem, vmem),
        scratch_shapes=[
            pltpu.VMEM((group, n, rows, width), f32),
            pltpu.VMEM((group - 1, n, rows, width), bf16),
            pltpu.VMEM((group - 1, n, rows, width), bf16),
            pltpu.VMEM((n, rows, width), bf16),
            pltpu.VMEM((per, full, width), bf16),
            pltpu.VMEM((per * full, full), bf16),
            pltpu.VMEM((group - 1, share, full), bf16),
            pltpu.VMEM((share, full), bf16),
            pltpu.VMEM((per * full, full), bf16),
            pltpu.VMEM((per, full, width), bf16),
            pltpu.VMEM((n, rows, width), bf16),
            dma((group,)),
            dma((group - 1,)),
            dma((group - 1,)),
            dma((owners - 1,)),
            dma((owners - 1,)),
            dma((group - 1,)),
            dma((group - 1,)),
            dma((group - 1,)),
            dma((group - 1,)),
            dma((owners - 1,)),
            dma((owners - 1,)),
            dma((2,)),
        ],
        compiler_params=pltpu.CompilerParams(
            collective_id=0, has_side_effects=True, vmem_limit_bytes=48 * 1024 * 1024
        ),
    )(grad_parts, momentum, live)


def per_device_step(mesh, grad_parts, momentum, layer_live):
    n, rows, width = momentum.shape
    owners = mesh.shape["dp"]
    group = mesh.shape["rep"] * mesh.shape["grp"]
    fits = (
        width % 128 == 0
        and rows % 16 == 0
        and n % owners == 0
        and (n // owners * owners * rows) % (16 * group) == 0
        and n * rows * width * group * 12 < 40 * 1024 * 1024
        and group > 1
        and owners > 1
    )
    if fits:
        return fused_step(mesh, grad_parts, momentum, layer_live)
    return per_device(grad_parts, momentum, layer_live)


def solution(mesh):
    placed = (P(("rep", "grp"), None, "dp", None), P(None, "dp", ("rep", "grp")), P())
    return jax.shard_map(
        functools.partial(per_device_step, mesh),
        mesh=mesh,
        in_specs=placed,
        out_specs=(P(None, "dp", ("rep", "grp")), P(None, "dp", ("rep", "grp"))),
        check_vma=False,
    )
```

```python
import functools
import math

import jax
import jax.numpy as jnp
from jax import lax
from jax.experimental import pallas as pl
from jax.experimental.pallas import tpu as pltpu
from jax.sharding import PartitionSpec as P

ITERS = 5


decay_rate = 0.95
first_coef = 3.4445
second_coef = -4.775
third_coef = 2.0315
norm_eps = 1e-07


def newton_schulz(source):
    source_f32 = source.astype(jnp.float32)
    frob_norm = jnp.sqrt(jnp.sum(source_f32 * source_f32))
    current = (source_f32 / (frob_norm + norm_eps)).astype(jnp.bfloat16)
    next_iterate = source_f32
    for iteration in range(ITERS):
        gram_matrix = lax.dot_general(
            current, current, (((1,), (1,)), ((), ())), preferred_element_type=jnp.float32
        ).astype(jnp.bfloat16)
        squared = jnp.dot(gram_matrix, gram_matrix, preferred_element_type=jnp.float32)
        polynomial = (second_coef * gram_matrix.astype(jnp.float32) + third_coef * squared).astype(
            jnp.bfloat16
        )
        next_iterate = first_coef * current.astype(jnp.float32) + jnp.dot(
            polynomial, current, preferred_element_type=jnp.float32
        )
        if iteration + 1 < ITERS:
            current = next_iterate.astype(jnp.bfloat16)
    return (next_iterate * math.sqrt(source.shape[1])).astype(jnp.bfloat16)


def zero_result(matrix):
    return jnp.zeros_like(matrix)


def guarded(matrix):
    return lax.cond(jnp.any(matrix != 0), newton_schulz, zero_result, matrix)


def per_device(grad_parts, momentum, layer_live):
    width = momentum.shape[2]
    col_start = lax.axis_index(("rep", "grp")) * width
    active = (layer_live > 0)[:, None, None]
    summed_share = lax.psum_scatter(grad_parts[0], ("rep", "grp"), scatter_dimension=2, tiled=True)
    fresh_momentum = jnp.where(active, decay_rate * momentum + summed_share, momentum)
    sources = lax.all_gather(
        fresh_momentum.astype(jnp.bfloat16), ("rep", "grp"), axis=2, tiled=True
    )
    owners = lax.axis_size("dp")
    matrices = layer_live.shape[0]
    per_owner = matrices // owners
    piece_rows = sources.shape[1]
    col_count = sources.shape[2]
    matrix_ids = jnp.arange(matrices, dtype=jnp.int32)
    live_flag = (layer_live > 0).astype(jnp.int32)
    slot_pos = matrix_ids % per_owner * owners + matrix_ids // per_owner
    slot_ids = jnp.arange(matrices, dtype=jnp.int32)
    placing = slot_pos[None, :] == slot_ids[:, None]
    holder = jnp.sum(jnp.where(placing, matrix_ids[None, :], 0), axis=1)
    filled = jnp.sum(placing.astype(jnp.int32) * live_flag[None, :], axis=1)
    picked_rows = jnp.take(sources, holder, axis=0)
    outgoing = jnp.where(filled[:, None, None] > 0, picked_rows, jnp.zeros_like(picked_rows))
    outgoing = outgoing.reshape(per_owner, owners, piece_rows, col_count)
    blocks = lax.all_to_all(outgoing, "dp", split_axis=1, concat_axis=1, tiled=True)
    item_count = blocks.shape[0]
    stacked = blocks.reshape(item_count, owners * piece_rows, col_count)
    results = lax.map(guarded, stacked)
    results = results.reshape(item_count, owners, piece_rows, col_count)
    returned = lax.all_to_all(results, "dp", split_axis=1, concat_axis=1, tiled=True)
    returned = returned.reshape(matrices, piece_rows, col_count)
    own_cols = lax.dynamic_slice_in_dim(returned, col_start, width, 2)
    gathered = jnp.take(own_cols, jnp.maximum(slot_pos, 0), axis=0)
    orth_update = jnp.where(active, gathered, jnp.zeros_like(gathered))
    return (fresh_momentum, orth_update)


MESH = pl.DeviceIdType.MESH


def split_dot(left, right):
    left_high = left.astype(jnp.bfloat16)
    left_low = (left - left_high.astype(jnp.float32)).astype(jnp.bfloat16)
    right_high = right.astype(jnp.bfloat16)
    right_low = (right - right_high.astype(jnp.float32)).astype(jnp.bfloat16)
    return (
        jnp.dot(left_high, right_high, preferred_element_type=jnp.float32)
        + jnp.dot(left_high, right_low, preferred_element_type=jnp.float32)
        + jnp.dot(left_low, right_high, preferred_element_type=jnp.float32)
    )


def f32_dot(left, right):
    return jnp.dot(
        left.astype(jnp.bfloat16), right.astype(jnp.bfloat16), preferred_element_type=jnp.float32
    )


gram_dot = f32_dot


def orthogonalizers(grams):
    rows = grams[0].shape[0]
    row_ids = lax.broadcasted_iota(jnp.int32, (rows, rows), 0)
    col_ids = lax.broadcasted_iota(jnp.int32, (rows, rows), 1)
    on_diag = row_ids == col_ids
    inverses, currents, products = [], [], [None] * len(grams)
    for gram in grams:
        diag = jnp.where(on_diag, gram, 0.0)
        squares = jnp.sum(jnp.sum(diag, axis=1, keepdims=True), axis=0, keepdims=True)
        inverse = 1.0 / (jnp.sqrt(squares) + norm_eps)
        inverses.append(inverse)
        currents.append(gram * inverse * inverse)
    for iteration in range(ITERS):
        highers = [
            second_coef * current + third_coef * gram_dot(current, current) for current in currents
        ]
        if iteration == 0:
            products = [jnp.where(on_diag, first_coef, 0.0) + higher for higher in highers]
        else:
            products = [
                first_coef * product + f32_dot(higher, product)
                for higher, product in zip(highers, products)
            ]
        if iteration + 1 < ITERS:
            halves = [
                first_coef * current + gram_dot(higher, current)
                for higher, current in zip(highers, currents)
            ]
            currents = [
                first_coef * half + gram_dot(higher, half) for higher, half in zip(highers, halves)
            ]
    return [product * inverse for product, inverse in zip(products, inverses)]


def step_kernel(
    sizes, grad_ref, mom_ref, live_ref, order_ref, slot_ref, new_ref, orth_ref,
    pbuf, prbuf, sbuf, rbuf, fresh, zsend, xbuf, gsend, grecv, gsum, gfull, osend, orecv,
    lsem, pssem, prsem, ssem, rsem, zssem, zrsem, gssem, grsem, assem, arsem, ossem, orsem, csem, *gbuf,
):
    group, owners, per_group, n, rows, width, slots = sizes
    per = -(-slots // owners)
    full = owners * rows
    share = per * full // group
    wire = gsend.dtype
    chips_x, chips_y = per_group // 2, group // per_group
    me_d = lax.axis_index("dp")
    me_y, me_g = lax.axis_index("rep"), lax.axis_index("grp")
    me_x, core = me_g // 2, lax.rem(me_g, 2)
    me = me_y * per_group + me_g
    hops = [(y, x) for y in range(chips_y) for x in range(chips_x)][::-1]

    def chip_id(hop, on):
        y = lax.rem(me_y + hop[0], chips_y)
        x = lax.rem(me_x + hop[1], chips_x)
        return {"rep": y, "grp": x * 2 + on}

    def peer_index(k):
        return lax.rem(me + k, group)

    def peer_id(k):
        peer = peer_index(k)
        return {"rep": peer // per_group, "grp": lax.rem(peer, per_group)}

    def owner_index(k):
        return lax.rem(me_d + k, owners)

    loads = []
    for k, hop in enumerate(hops):
        for side, on in ((1, 1 - core), (0, core)):
            place = chip_id(hop, on)
            start = pl.multiple_of((place["rep"] * per_group + place["grp"]) * width, width)
            load = pltpu.make_async_copy(
                grad_ref.at[0, :, :, pl.ds(start, width)],
                gbuf[2 * k + side],
                lsem.at[2 * k + side],
            )
            load.start()
            loads.append(load)
    barrier = pltpu.get_barrier_semaphore()
    for k in range(1, group):
        pl.semaphore_signal(barrier, inc=1, device_id=peer_id(k), device_id_type=MESH)
    for k in range(1, owners):
        pl.semaphore_signal(barrier, inc=1, device_id={"dp": owner_index(k)}, device_id_type=MESH)
    pl.semaphore_wait(barrier, group + owners - 2)

    psends = []
    for k in range(len(hops)):
        loads[2 * k].wait()
        for s in range(slots):
            pbuf[k, s] = gbuf[2 * k + 1][order_ref[s]].astype(jnp.bfloat16)
        copy = pltpu.make_async_remote_copy(
            src_ref=pbuf.at[k], dst_ref=prbuf.at[k],
            send_sem=pssem.at[k], recv_sem=prsem.at[k],
            device_id={"grp": me_x * 2 + 1 - core}, device_id_type=MESH,
        )
        copy.start()
        psends.append(copy)
    sends = []
    for k, hop in enumerate(hops[:-1]):
        loads[2 * k + 1].wait()
        psends[k].wait_recv()
        for s in range(slots):
            pair = gbuf[2 * k][order_ref[s]] + prbuf[k, s].astype(jnp.float32)
            sbuf[k, s] = pair.astype(jnp.bfloat16)
        copy = pltpu.make_async_remote_copy(
            src_ref=sbuf.at[k], dst_ref=rbuf.at[k],
            send_sem=ssem.at[k], recv_sem=rsem.at[k],
            device_id=chip_id(hop, core), device_id_type=MESH,
        )
        copy.start()
        sends.append(copy)
    last = len(hops) - 1
    loads[2 * last + 1].wait()
    psends[last].wait_recv()
    for s in range(slots):
        held = gbuf[2 * last][order_ref[s]] + prbuf[last, s].astype(jnp.float32)
        fresh[s] = held + decay_rate * mom_ref[order_ref[s]]
    for s in range(slots, owners * per):
        zsend[s] = jnp.zeros((rows, width), jnp.bfloat16)
    for copy in sends:
        copy.wait_recv()
    for s in range(slots):
        total = fresh[s]
        for k in range(last):
            total = total + rbuf[k, s].astype(jnp.float32)
        fresh[s] = total
        zsend[s] = total.astype(jnp.bfloat16)

    my_rows = pl.ds(pl.multiple_of(me_d * rows, rows), rows)
    own = pltpu.make_async_copy(
        zsend.at[pl.ds(me_d * per, per)], xbuf.at[:, my_rows, :], csem.at[0]
    )
    own.start()
    zcopies = []
    for k in range(1, owners):
        copy = pltpu.make_async_remote_copy(
            src_ref=zsend.at[pl.ds(owner_index(k) * per, per)], dst_ref=xbuf.at[:, my_rows, :],
            send_sem=zssem.at[k - 1], recv_sem=zrsem.at[k - 1],
            device_id={"dp": owner_index(k)}, device_id_type=MESH,
        )
        copy.start()
        zcopies.append(copy)
    for i in range(n):
        new_ref[i] = jnp.where(live_ref[i] > 0, fresh[slot_ref[i]], mom_ref[i])
    own.wait()
    for copy in zcopies:
        copy.wait_recv()

    for m in range(per):
        block = xbuf[m]
        gram = lax.dot_general(
            block, block, (((1,), (1,)), ((), ())), preferred_element_type=jnp.float32
        )
        gsend[m * full : (m + 1) * full] = gram.astype(wire)
    gcopies = []
    for k in range(1, group):
        start = pl.multiple_of(peer_index(k) * share, share)
        copy = pltpu.make_async_remote_copy(
            src_ref=gsend.at[pl.ds(start, share)], dst_ref=grecv.at[k - 1],
            send_sem=gssem.at[k - 1], recv_sem=grsem.at[k - 1],
            device_id=peer_id(k), device_id_type=MESH,
        )
        copy.start()
        gcopies.append(copy)
    my_share = pl.ds(pl.multiple_of(me * share, share), share)
    total = gsend[my_share].astype(jnp.float32)
    for k in range(1, group):
        gcopies[k - 1].wait_recv()
        total = total + grecv[k - 1].astype(jnp.float32)
    gsum[...] = total.astype(wire)
    acopies = []
    for k in range(1, group):
        copy = pltpu.make_async_remote_copy(
            src_ref=gsum, dst_ref=gfull.at[my_share],
            send_sem=assem.at[k - 1], recv_sem=arsem.at[k - 1],
            device_id=peer_id(k), device_id_type=MESH,
        )
        copy.start()
        acopies.append(copy)
    gfull[my_share] = gsum[...]
    for copy in acopies:
        copy.wait_recv()

    scale = math.sqrt(width * group)
    factors = orthogonalizers(
        [gfull[m * full : (m + 1) * full].astype(jnp.float32) for m in range(per)]
    )
    for m in range(per):
        osend[m] = f32_dot(factors[m] * scale, xbuf[m]).astype(jnp.bfloat16)
    own = pltpu.make_async_copy(
        osend.at[:, my_rows, :], orecv.at[pl.ds(me_d * per, per)], csem.at[1]
    )
    own.start()
    ocopies = []
    for k in range(1, owners):
        their_rows = pl.ds(pl.multiple_of(owner_index(k) * rows, rows), rows)
        copy = pltpu.make_async_remote_copy(
            src_ref=osend.at[:, their_rows, :], dst_ref=orecv.at[pl.ds(me_d * per, per)],
            send_sem=ossem.at[k - 1], recv_sem=orsem.at[k - 1],
            device_id={"dp": owner_index(k)}, device_id_type=MESH,
        )
        copy.start()
        ocopies.append(copy)
    for copies in (psends, sends, zcopies, gcopies, acopies):
        for copy in copies:
            copy.wait_send()
    own.wait()
    for copy in ocopies:
        copy.wait_recv()
    for i in range(n):
        part = orecv[slot_ref[i]]
        orth_ref[i] = jnp.where(live_ref[i] > 0, part.astype(jnp.float32), 0.0).astype(jnp.bfloat16)
    for copy in ocopies:
        copy.wait_send()


def fused_step(mesh, slots, number, grad_parts, momentum, live, order, slot):
    n, rows, width = momentum.shape
    owners, per_group = mesh.shape["dp"], mesh.shape["grp"]
    group = mesh.shape["rep"] * per_group
    chips = group // 2
    per = -(-slots // owners)
    full = owners * rows
    share = per * full // group
    bf16, f32 = jnp.bfloat16, jnp.float32
    wire = bf16 if share % 16 == 0 else f32
    dma = pltpu.SemaphoreType.DMA
    vmem = pl.BlockSpec(memory_space=pltpu.VMEM)
    smem = pl.BlockSpec(memory_space=pltpu.SMEM)
    return pl.pallas_call(
        functools.partial(step_kernel, (group, owners, per_group, n, rows, width, slots)),
        out_shape=(
            jax.ShapeDtypeStruct((n, rows, width), f32),
            jax.ShapeDtypeStruct((n, rows, width), bf16),
        ),
        in_specs=[pl.BlockSpec(memory_space=pl.ANY), vmem, vmem, smem, smem],
        out_specs=(vmem, vmem),
        scratch_shapes=[
            pltpu.VMEM((chips, slots, rows, width), bf16),
            pltpu.VMEM((chips, slots, rows, width), bf16),
            pltpu.VMEM((chips - 1, slots, rows, width), bf16),
            pltpu.VMEM((chips - 1, slots, rows, width), bf16),
            pltpu.VMEM((slots, rows, width), f32),
            pltpu.VMEM((owners * per, rows, width), bf16),
            pltpu.VMEM((per, full, width), bf16),
            pltpu.VMEM((per * full, full), wire),
            pltpu.VMEM((group - 1, share, full), wire),
            pltpu.VMEM((share, full), wire),
            pltpu.VMEM((per * full, full), wire),
            pltpu.VMEM((per, full, width), bf16),
            pltpu.VMEM((owners * per, rows, width), bf16),
            dma((group,)),
            dma((chips,)),
            dma((chips,)),
            dma((chips - 1,)),
            dma((chips - 1,)),
            dma((owners - 1,)),
            dma((owners - 1,)),
            dma((group - 1,)),
            dma((group - 1,)),
            dma((group - 1,)),
            dma((group - 1,)),
            dma((owners - 1,)),
            dma((owners - 1,)),
            dma((2,)),
            *[pltpu.VMEM((n, rows, width), f32) for _ in range(group)],
        ],
        compiler_params=pltpu.CompilerParams(
            collective_id=number, has_side_effects=True, vmem_limit_bytes=48 * 1024 * 1024
        ),
    )(grad_parts, momentum, live, order, slot)


def per_device_step(mesh, grad_parts, momentum, layer_live):
    n, rows, width = momentum.shape
    owners, per_group = mesh.shape["dp"], mesh.shape["grp"]
    group = mesh.shape["rep"] * per_group
    fits = (
        width % 128 == 0
        and rows % 16 == 0
        and (owners * rows) % (8 * group) == 0
        and n * rows * width * group * 12 < 40 * 1024 * 1024
        and per_group % 2 == 0
        and group > 2
        and owners > 1
    )
    if not fits:
        return per_device(grad_parts, momentum, layer_live)
    flags = (layer_live > 0).astype(jnp.int32)
    before = jnp.cumsum(flags) - flags
    count = jnp.sum(flags)
    ids = jnp.arange(n, dtype=jnp.int32)
    slot = jnp.where(flags > 0, before, count + ids - before)
    order = jnp.sum(jnp.where(slot[None, :] == ids[:, None], ids[None, :], 0), axis=1)
    live = jnp.broadcast_to(flags.astype(jnp.float32)[:, None, None], (n, 1, width))
    sizes = sorted({-(-n * part // 8) for part in (2, 3, 4, 5, 6, 8)})
    index = sum((count > size).astype(jnp.int32) for size in sizes[:-1])
    branches = [
        functools.partial(fused_step, mesh, size, number) for number, size in enumerate(sizes)
    ]
    room = jnp.asarray(sizes, jnp.int32)[index]
    slot = jnp.minimum(slot, room - 1)
    return lax.switch(index, branches, grad_parts, momentum, live, order, slot)


def solution(mesh):
    placed = (P(("rep", "grp"), None, "dp", None), P(None, "dp", ("rep", "grp")), P())
    return jax.shard_map(
        functools.partial(per_device_step, mesh),
        mesh=mesh,
        in_specs=placed,
        out_specs=(P(None, "dp", ("rep", "grp")), P(None, "dp", ("rep", "grp"))),
        check_vma=False,
    )
```

```python
import functools
import math

import jax
import jax.numpy as jnp
from jax import lax
from jax.experimental import pallas as pl
from jax.experimental.pallas import tpu as pltpu
from jax.sharding import PartitionSpec as P

ITERS = 5


decay_rate = 0.95
first_coef = 3.4445
second_coef = -4.775
third_coef = 2.0315
norm_eps = 1e-07


def newton_schulz(source):
    source_f32 = source.astype(jnp.float32)
    frob_norm = jnp.sqrt(jnp.sum(source_f32 * source_f32))
    current = (source_f32 / (frob_norm + norm_eps)).astype(jnp.bfloat16)
    next_iterate = source_f32
    for iteration in range(ITERS):
        gram_matrix = lax.dot_general(
            current, current, (((1,), (1,)), ((), ())), preferred_element_type=jnp.float32
        ).astype(jnp.bfloat16)
        squared = jnp.dot(gram_matrix, gram_matrix, preferred_element_type=jnp.float32)
        polynomial = (second_coef * gram_matrix.astype(jnp.float32) + third_coef * squared).astype(
            jnp.bfloat16
        )
        next_iterate = first_coef * current.astype(jnp.float32) + jnp.dot(
            polynomial, current, preferred_element_type=jnp.float32
        )
        if iteration + 1 < ITERS:
            current = next_iterate.astype(jnp.bfloat16)
    return (next_iterate * math.sqrt(source.shape[1])).astype(jnp.bfloat16)


def zero_result(matrix):
    return jnp.zeros_like(matrix)


def guarded(matrix):
    return lax.cond(jnp.any(matrix != 0), newton_schulz, zero_result, matrix)


def per_device(grad_parts, momentum, layer_live):
    width = momentum.shape[2]
    col_start = lax.axis_index(("rep", "grp")) * width
    active = (layer_live > 0)[:, None, None]
    summed_share = lax.psum_scatter(grad_parts[0], ("rep", "grp"), scatter_dimension=2, tiled=True)
    fresh_momentum = jnp.where(active, decay_rate * momentum + summed_share, momentum)
    sources = lax.all_gather(
        fresh_momentum.astype(jnp.bfloat16), ("rep", "grp"), axis=2, tiled=True
    )
    owners = lax.axis_size("dp")
    matrices = layer_live.shape[0]
    per_owner = matrices // owners
    piece_rows = sources.shape[1]
    col_count = sources.shape[2]
    matrix_ids = jnp.arange(matrices, dtype=jnp.int32)
    live_flag = (layer_live > 0).astype(jnp.int32)
    slot_pos = matrix_ids % per_owner * owners + matrix_ids // per_owner
    slot_ids = jnp.arange(matrices, dtype=jnp.int32)
    placing = slot_pos[None, :] == slot_ids[:, None]
    holder = jnp.sum(jnp.where(placing, matrix_ids[None, :], 0), axis=1)
    filled = jnp.sum(placing.astype(jnp.int32) * live_flag[None, :], axis=1)
    picked_rows = jnp.take(sources, holder, axis=0)
    outgoing = jnp.where(filled[:, None, None] > 0, picked_rows, jnp.zeros_like(picked_rows))
    outgoing = outgoing.reshape(per_owner, owners, piece_rows, col_count)
    blocks = lax.all_to_all(outgoing, "dp", split_axis=1, concat_axis=1, tiled=True)
    item_count = blocks.shape[0]
    stacked = blocks.reshape(item_count, owners * piece_rows, col_count)
    results = lax.map(guarded, stacked)
    results = results.reshape(item_count, owners, piece_rows, col_count)
    returned = lax.all_to_all(results, "dp", split_axis=1, concat_axis=1, tiled=True)
    returned = returned.reshape(matrices, piece_rows, col_count)
    own_cols = lax.dynamic_slice_in_dim(returned, col_start, width, 2)
    gathered = jnp.take(own_cols, jnp.maximum(slot_pos, 0), axis=0)
    orth_update = jnp.where(active, gathered, jnp.zeros_like(gathered))
    return (fresh_momentum, orth_update)


MESH = pl.DeviceIdType.MESH


def f32_dot(left, right):
    return jnp.dot(
        left.astype(jnp.bfloat16), right.astype(jnp.bfloat16), preferred_element_type=jnp.float32
    )


def orthogonalizers(grams):
    rows = grams[0].shape[0]
    row_ids = lax.broadcasted_iota(jnp.int32, (rows, rows), 0)
    col_ids = lax.broadcasted_iota(jnp.int32, (rows, rows), 1)
    on_diag = row_ids == col_ids

    def less(matrix, shift):
        return jnp.where(on_diag, matrix - shift, matrix)

    inverses, currents = [], []
    for gram in grams:
        diag = jnp.where(on_diag, gram, 0.0)
        squares = jnp.sum(jnp.sum(diag, axis=1, keepdims=True), axis=0, keepdims=True)
        inverse = 1.0 / (jnp.sqrt(squares) + norm_eps)
        inverses.append(inverse)
        currents.append(gram * inverse * inverse)
    level, product_level = 1.0 / rows, 1.0
    products = [None] * len(grams)
    for iteration in range(ITERS):
        gain = second_coef * level + third_coef * level * level
        scale = first_coef + gain
        half_level = scale * level
        for m, current in enumerate(currents):
            rest = less(current, level)
            square = level * (current + rest) + f32_dot(rest, rest)
            change = less(second_coef * current + third_coef * square, gain)
            if iteration == 0:
                products[m] = less(change, -scale)
            else:
                products[m] = (
                    scale * products[m]
                    + product_level * change
                    + f32_dot(change, less(products[m], product_level))
                )
            if iteration + 1 < ITERS:
                half = scale * current + level * change + f32_dot(change, rest)
                currents[m] = (
                    scale * half
                    + half_level * change
                    + f32_dot(change, less(half, half_level))
                )
        product_level = scale * product_level
        level = scale * half_level
    return [product * inverse for product, inverse in zip(products, inverses)]


def step_kernel(
    sizes, grad_ref, momentum_ref, live_ref, new_hbm, orth_ref,
    mom_ref, new_ref, pbuf, prbuf, sbuf, rbuf, fresh, zsend, xbuf, gsend, gpair, ghalf, gchip, gsum, gfull, osend, orecv,
    lsem, pssem, prsem, ssem, rsem, zssem, zrsem, gssem, grsem, hsem, ossem, orsem, csem, *gbuf,
):
    group, owners, per_group, n, rows, width, slots = sizes
    per = -(-slots // owners)
    full = owners * rows
    half = per * full // 2
    chips_x, chips_y = per_group // 2, group // per_group
    me_d = lax.axis_index("dp")
    me_y, me_g = lax.axis_index("rep"), lax.axis_index("grp")
    me_x, core = me_g // 2, lax.rem(me_g, 2)
    me = me_y * per_group + me_g
    hops = [(y, x) for y in range(chips_y) for x in range(chips_x)][::-1]

    def chip_id(hop, on):
        y = lax.rem(me_y + hop[0], chips_y)
        x = lax.rem(me_x + hop[1], chips_x)
        return {"rep": y, "grp": x * 2 + on}

    def peer_index(k):
        return lax.rem(me + k, group)

    def peer_id(k):
        peer = peer_index(k)
        return {"rep": peer // per_group, "grp": lax.rem(peer, per_group)}

    def owner_index(k):
        return lax.rem(me_d + k, owners)

    loads = []
    for k, hop in enumerate(hops):
        for side, on in ((1, 1 - core), (0, core)):
            place = chip_id(hop, on)
            start = pl.multiple_of((place["rep"] * per_group + place["grp"]) * width, width)
            load = pltpu.make_async_copy(
                grad_ref.at[0, :, :, pl.ds(start, width)],
                gbuf[2 * k + side],
                lsem.at[2 * k + side],
            )
            load.start()
            loads.append(load)
    mom_load = pltpu.make_async_copy(momentum_ref, mom_ref, csem.at[2])
    mom_load.start()
    flags = [jnp.where(live_ref[i] > 0, 1, 0) for i in range(n)]
    count = sum(flags)
    slot, before = [], 0
    for i in range(n):
        slot.append(jnp.where(flags[i] > 0, before, count + i - before))
        before = before + flags[i]
    order = [sum(jnp.where(slot[i] == s, i, 0) for i in range(n)) for s in range(slots)]
    slot = [jnp.minimum(place, slots - 1) for place in slot]
    barrier = pltpu.get_barrier_semaphore()
    for k in range(1, group):
        pl.semaphore_signal(barrier, inc=1, device_id=peer_id(k), device_id_type=MESH)
    for k in range(1, owners):
        pl.semaphore_signal(barrier, inc=1, device_id={"dp": owner_index(k)}, device_id_type=MESH)
    pl.semaphore_wait(barrier, group + owners - 2)

    psends = []
    for k in range(len(hops)):
        loads[2 * k].wait()
        for s in range(slots):
            pbuf[k, s] = gbuf[2 * k + 1][order[s]].astype(jnp.bfloat16)
        copy = pltpu.make_async_remote_copy(
            src_ref=pbuf.at[k], dst_ref=prbuf.at[k],
            send_sem=pssem.at[k], recv_sem=prsem.at[k],
            device_id={"grp": me_x * 2 + 1 - core}, device_id_type=MESH,
        )
        copy.start()
        psends.append(copy)
    sends = []
    for k, hop in enumerate(hops[:-1]):
        loads[2 * k + 1].wait()
        psends[k].wait_recv()
        for s in range(slots):
            pair = gbuf[2 * k][order[s]] + prbuf[k, s].astype(jnp.float32)
            sbuf[k, s] = pair.astype(jnp.bfloat16)
        copy = pltpu.make_async_remote_copy(
            src_ref=sbuf.at[k], dst_ref=rbuf.at[k],
            send_sem=ssem.at[k], recv_sem=rsem.at[k],
            device_id=chip_id(hop, core), device_id_type=MESH,
        )
        copy.start()
        sends.append(copy)
    last = len(hops) - 1
    loads[2 * last + 1].wait()
    psends[last].wait_recv()
    mom_load.wait()
    for s in range(slots):
        held = gbuf[2 * last][order[s]] + prbuf[last, s].astype(jnp.float32)
        fresh[s] = held + decay_rate * mom_ref[order[s]]
    for s in range(slots, owners * per):
        zsend[s] = jnp.zeros((rows, width), jnp.bfloat16)
    for copy in sends:
        copy.wait_recv()
    for s in range(slots):
        total = fresh[s]
        for k in range(last):
            total = total + rbuf[k, s].astype(jnp.float32)
        fresh[s] = total
        zsend[s] = total.astype(jnp.bfloat16)

    my_rows = pl.ds(pl.multiple_of(me_d * rows, rows), rows)
    own = pltpu.make_async_copy(
        zsend.at[pl.ds(me_d * per, per)], xbuf.at[:, my_rows, :], csem.at[0]
    )
    own.start()
    zcopies = []
    for k in range(1, owners):
        copy = pltpu.make_async_remote_copy(
            src_ref=zsend.at[pl.ds(owner_index(k) * per, per)], dst_ref=xbuf.at[:, my_rows, :],
            send_sem=zssem.at[k - 1], recv_sem=zrsem.at[k - 1],
            device_id={"dp": owner_index(k)}, device_id_type=MESH,
        )
        copy.start()
        zcopies.append(copy)
    alive = [jnp.full((1, width), flag, jnp.int32) > 0 for flag in flags]
    for i in range(n):
        new_ref[i] = jnp.where(alive[i], fresh[slot[i]], mom_ref[i])
    new_store = pltpu.make_async_copy(new_ref, new_hbm, csem.at[3])
    new_store.start()
    own.wait()
    for copy in zcopies:
        copy.wait_recv()

    for m in range(per):
        block = xbuf[m]
        gram = lax.dot_general(
            block, block, (((1,), (1,)), ((), ())), preferred_element_type=jnp.float32
        )
        gsend[m * full : (m + 1) * full] = gram.astype(jnp.bfloat16)
    my_half = pl.ds(pl.multiple_of(core * half, half), half)
    their_half = pl.ds(pl.multiple_of((1 - core) * half, half), half)
    partner = {"grp": me_x * 2 + 1 - core}
    to_pair = pltpu.make_async_remote_copy(
        src_ref=gsend.at[their_half], dst_ref=gpair,
        send_sem=hsem.at[0], recv_sem=hsem.at[1], device_id=partner, device_id_type=MESH,
    )
    to_pair.start()
    to_pair.wait_recv()
    total = gsend[my_half].astype(jnp.float32) + gpair[...].astype(jnp.float32)
    ghalf[...] = total.astype(jnp.bfloat16)
    gcopies = []
    for k, hop in enumerate(hops[:-1]):
        copy = pltpu.make_async_remote_copy(
            src_ref=ghalf, dst_ref=gchip.at[k],
            send_sem=gssem.at[k], recv_sem=grsem.at[k],
            device_id=chip_id(hop, core), device_id_type=MESH,
        )
        copy.start()
        gcopies.append(copy)
    for copy in gcopies:
        copy.wait_recv()
    for k in range(last):
        total = total + gchip[k].astype(jnp.float32)
    gsum[...] = total.astype(jnp.bfloat16)
    to_both = pltpu.make_async_remote_copy(
        src_ref=gsum, dst_ref=gfull.at[my_half],
        send_sem=hsem.at[2], recv_sem=hsem.at[3], device_id=partner, device_id_type=MESH,
    )
    to_both.start()
    gfull[my_half] = gsum[...]
    to_both.wait_recv()

    scale = math.sqrt(width * group)
    factors = orthogonalizers(
        [gfull[m * full : (m + 1) * full].astype(jnp.float32) for m in range(per)]
    )
    for m in range(per):
        osend[m] = f32_dot(factors[m] * scale, xbuf[m]).astype(jnp.bfloat16)
    own = pltpu.make_async_copy(
        osend.at[:, my_rows, :], orecv.at[pl.ds(me_d * per, per)], csem.at[1]
    )
    own.start()
    ocopies = []
    for k in range(1, owners):
        their_rows = pl.ds(pl.multiple_of(owner_index(k) * rows, rows), rows)
        copy = pltpu.make_async_remote_copy(
            src_ref=osend.at[:, their_rows, :], dst_ref=orecv.at[pl.ds(me_d * per, per)],
            send_sem=ossem.at[k - 1], recv_sem=orsem.at[k - 1],
            device_id={"dp": owner_index(k)}, device_id_type=MESH,
        )
        copy.start()
        ocopies.append(copy)
    for copies in (psends, sends, zcopies, gcopies, [to_pair, to_both]):
        for copy in copies:
            copy.wait_send()
    own.wait()
    for copy in ocopies:
        copy.wait_recv()
    for i in range(n):
        part = orecv[slot[i]]
        orth_ref[i] = jnp.where(alive[i], part.astype(jnp.float32), 0.0).astype(jnp.bfloat16)
    for copy in ocopies:
        copy.wait_send()
    new_store.wait()


def fused_step(mesh, slots, number, grad_parts, momentum, live):
    n, rows, width = momentum.shape
    owners, per_group = mesh.shape["dp"], mesh.shape["grp"]
    group = mesh.shape["rep"] * per_group
    chips = group // 2
    per = -(-slots // owners)
    full = owners * rows
    half = per * full // 2
    bf16, f32 = jnp.bfloat16, jnp.float32
    dma = pltpu.SemaphoreType.DMA
    vmem = pl.BlockSpec(memory_space=pltpu.VMEM)
    smem = pl.BlockSpec(memory_space=pltpu.SMEM)
    hbm = pl.BlockSpec(memory_space=pl.ANY)
    return pl.pallas_call(
        functools.partial(step_kernel, (group, owners, per_group, n, rows, width, slots)),
        out_shape=(
            jax.ShapeDtypeStruct((n, rows, width), f32),
            jax.ShapeDtypeStruct((n, rows, width), bf16),
        ),
        in_specs=[hbm, hbm, smem],
        out_specs=(hbm, vmem),
        scratch_shapes=[
            pltpu.VMEM((n, rows, width), f32),
            pltpu.VMEM((n, rows, width), f32),
            pltpu.VMEM((chips, slots, rows, width), bf16),
            pltpu.VMEM((chips, slots, rows, width), bf16),
            pltpu.VMEM((chips - 1, slots, rows, width), bf16),
            pltpu.VMEM((chips - 1, slots, rows, width), bf16),
            pltpu.VMEM((slots, rows, width), f32),
            pltpu.VMEM((owners * per, rows, width), bf16),
            pltpu.VMEM((per, full, width), bf16),
            pltpu.VMEM((per * full, full), bf16),
            pltpu.VMEM((half, full), bf16),
            pltpu.VMEM((half, full), bf16),
            pltpu.VMEM((chips - 1, half, full), bf16),
            pltpu.VMEM((half, full), bf16),
            pltpu.VMEM((per * full, full), bf16),
            pltpu.VMEM((per, full, width), bf16),
            pltpu.VMEM((owners * per, rows, width), bf16),
            dma((group,)),
            dma((chips,)),
            dma((chips,)),
            dma((chips - 1,)),
            dma((chips - 1,)),
            dma((owners - 1,)),
            dma((owners - 1,)),
            dma((chips - 1,)),
            dma((chips - 1,)),
            dma((4,)),
            dma((owners - 1,)),
            dma((owners - 1,)),
            dma((4,)),
            *[pltpu.VMEM((n, rows, width), f32) for _ in range(group)],
        ],
        compiler_params=pltpu.CompilerParams(
            collective_id=number, has_side_effects=True, vmem_limit_bytes=48 * 1024 * 1024
        ),
    )(grad_parts, momentum, live)


def per_device_step(mesh, grad_parts, momentum, layer_live):
    n, rows, width = momentum.shape
    owners, per_group = mesh.shape["dp"], mesh.shape["grp"]
    group = mesh.shape["rep"] * per_group
    fits = (
        width % 128 == 0
        and rows % 16 == 0
        and (owners * rows) % 32 == 0
        and n * rows * width * group * 12 < 40 * 1024 * 1024
        and per_group % 2 == 0
        and group > 2
        and owners > 1
    )
    if not fits:
        return per_device(grad_parts, momentum, layer_live)
    count = jnp.sum((layer_live > 0).astype(jnp.int32))
    sizes = sorted({-(-n * part // 8) for part in (2, 3, 4, 5, 6, 8)})
    index = sum((count > size).astype(jnp.int32) for size in sizes[:-1])
    branches = [
        functools.partial(fused_step, mesh, size, number) for number, size in enumerate(sizes)
    ]
    return lax.switch(index, branches, grad_parts, momentum, layer_live)


def solution(mesh):
    placed = (P(("rep", "grp"), None, "dp", None), P(None, "dp", ("rep", "grp")), P())
    return jax.shard_map(
        functools.partial(per_device_step, mesh),
        mesh=mesh,
        in_specs=placed,
        out_specs=(P(None, "dp", ("rep", "grp")), P(None, "dp", ("rep", "grp"))),
        check_vma=False,
    )
```

```python
import functools
import math

import jax
import jax.numpy as jnp
from jax import lax
from jax.experimental import pallas as pl
from jax.experimental.pallas import tpu as pltpu
from jax.sharding import PartitionSpec as P

ITERS = 5


decay_rate = 0.95
first_coef = 3.4445
second_coef = -4.775
third_coef = 2.0315
norm_eps = 1e-07


def newton_schulz(source):
    source_f32 = source.astype(jnp.float32)
    frob_norm = jnp.sqrt(jnp.sum(source_f32 * source_f32))
    current = (source_f32 / (frob_norm + norm_eps)).astype(jnp.bfloat16)
    next_iterate = source_f32
    for iteration in range(ITERS):
        gram_matrix = lax.dot_general(
            current, current, (((1,), (1,)), ((), ())), preferred_element_type=jnp.float32
        ).astype(jnp.bfloat16)
        squared = jnp.dot(gram_matrix, gram_matrix, preferred_element_type=jnp.float32)
        polynomial = (second_coef * gram_matrix.astype(jnp.float32) + third_coef * squared).astype(
            jnp.bfloat16
        )
        next_iterate = first_coef * current.astype(jnp.float32) + jnp.dot(
            polynomial, current, preferred_element_type=jnp.float32
        )
        if iteration + 1 < ITERS:
            current = next_iterate.astype(jnp.bfloat16)
    return (next_iterate * math.sqrt(source.shape[1])).astype(jnp.bfloat16)


def zero_result(matrix):
    return jnp.zeros_like(matrix)


def guarded(matrix):
    return lax.cond(jnp.any(matrix != 0), newton_schulz, zero_result, matrix)


def per_device(grad_parts, momentum, layer_live):
    width = momentum.shape[2]
    col_start = lax.axis_index(("rep", "grp")) * width
    active = (layer_live > 0)[:, None, None]
    summed_share = lax.psum_scatter(grad_parts[0], ("rep", "grp"), scatter_dimension=2, tiled=True)
    fresh_momentum = jnp.where(active, decay_rate * momentum + summed_share, momentum)
    sources = lax.all_gather(
        fresh_momentum.astype(jnp.bfloat16), ("rep", "grp"), axis=2, tiled=True
    )
    owners = lax.axis_size("dp")
    matrices = layer_live.shape[0]
    per_owner = matrices // owners
    piece_rows = sources.shape[1]
    col_count = sources.shape[2]
    matrix_ids = jnp.arange(matrices, dtype=jnp.int32)
    live_flag = (layer_live > 0).astype(jnp.int32)
    slot_pos = matrix_ids % per_owner * owners + matrix_ids // per_owner
    slot_ids = jnp.arange(matrices, dtype=jnp.int32)
    placing = slot_pos[None, :] == slot_ids[:, None]
    holder = jnp.sum(jnp.where(placing, matrix_ids[None, :], 0), axis=1)
    filled = jnp.sum(placing.astype(jnp.int32) * live_flag[None, :], axis=1)
    picked_rows = jnp.take(sources, holder, axis=0)
    outgoing = jnp.where(filled[:, None, None] > 0, picked_rows, jnp.zeros_like(picked_rows))
    outgoing = outgoing.reshape(per_owner, owners, piece_rows, col_count)
    blocks = lax.all_to_all(outgoing, "dp", split_axis=1, concat_axis=1, tiled=True)
    item_count = blocks.shape[0]
    stacked = blocks.reshape(item_count, owners * piece_rows, col_count)
    results = lax.map(guarded, stacked)
    results = results.reshape(item_count, owners, piece_rows, col_count)
    returned = lax.all_to_all(results, "dp", split_axis=1, concat_axis=1, tiled=True)
    returned = returned.reshape(matrices, piece_rows, col_count)
    own_cols = lax.dynamic_slice_in_dim(returned, col_start, width, 2)
    gathered = jnp.take(own_cols, jnp.maximum(slot_pos, 0), axis=0)
    orth_update = jnp.where(active, gathered, jnp.zeros_like(gathered))
    return (fresh_momentum, orth_update)


MESH = pl.DeviceIdType.MESH


def f32_dot(left, right):
    return jnp.dot(
        left.astype(jnp.bfloat16), right.astype(jnp.bfloat16), preferred_element_type=jnp.float32
    )


def orthogonalizers(grams):
    rows = grams[0].shape[0]
    row_ids = lax.broadcasted_iota(jnp.int32, (rows, rows), 0)
    col_ids = lax.broadcasted_iota(jnp.int32, (rows, rows), 1)
    on_diag = row_ids == col_ids

    def less(matrix, shift):
        return jnp.where(on_diag, matrix - shift, matrix)

    inverses, currents = [], []
    for gram in grams:
        diag = jnp.where(on_diag, gram, 0.0)
        squares = jnp.sum(jnp.sum(diag, axis=1, keepdims=True), axis=0, keepdims=True)
        inverse = 1.0 / (jnp.sqrt(squares) + norm_eps)
        inverses.append(inverse)
        currents.append(gram * inverse * inverse)
    level, product_level = 1.0 / rows, 1.0
    products = [None] * len(grams)
    for iteration in range(ITERS):
        gain = second_coef * level + third_coef * level * level
        scale = first_coef + gain
        half_level = scale * level
        for m, current in enumerate(currents):
            rest = less(current, level)
            square = level * (current + rest) + f32_dot(rest, rest)
            change = less(second_coef * current + third_coef * square, gain)
            if iteration == 0:
                products[m] = less(change, -scale)
            else:
                products[m] = (
                    scale * products[m]
                    + product_level * change
                    + f32_dot(change, less(products[m], product_level))
                )
            if iteration + 1 < ITERS:
                half = scale * current + level * change + f32_dot(change, rest)
                currents[m] = (
                    scale * half
                    + half_level * change
                    + f32_dot(change, less(half, half_level))
                )
        product_level = scale * product_level
        level = scale * half_level
    return [product * inverse for product, inverse in zip(products, inverses)]


def step_kernel(
    sizes, grad_ref, momentum_ref, live_ref, new_hbm, orth_ref,
    mom_ref, new_ref, pbuf, prbuf, sbuf, rbuf, fresh, zsend, xbuf, gsend, gpair, ghalf, gchip, gsum, gfull, osend, orecv,
    lsem, pssem, prsem, ssem, rsem, zssem, zrsem, gssem, grsem, hsem, ossem, orsem, csem, *gbuf,
):
    group, owners, per_group, n, rows, width, slots = sizes
    per = -(-slots // owners)
    full = owners * rows
    half = per * full // 2
    chips_x, chips_y = per_group // 2, group // per_group
    me_d = lax.axis_index("dp")
    me_y, me_g = lax.axis_index("rep"), lax.axis_index("grp")
    me_x, core = me_g // 2, lax.rem(me_g, 2)
    me = me_y * per_group + me_g
    hops = [(y, x) for y in range(chips_y) for x in range(chips_x)][::-1]

    def chip_id(hop, on):
        y = lax.rem(me_y + hop[0], chips_y)
        x = lax.rem(me_x + hop[1], chips_x)
        return {"rep": y, "grp": x * 2 + on}

    def peer_index(k):
        return lax.rem(me + k, group)

    def peer_id(k):
        peer = peer_index(k)
        return {"rep": peer // per_group, "grp": lax.rem(peer, per_group)}

    def owner_index(k):
        return lax.rem(me_d + k, owners)

    loads = []
    for k, hop in enumerate(hops):
        for side, on in ((1, 1 - core), (0, core)):
            place = chip_id(hop, on)
            start = pl.multiple_of((place["rep"] * per_group + place["grp"]) * width, width)
            load = pltpu.make_async_copy(
                grad_ref.at[0, :, :, pl.ds(start, width)],
                gbuf[2 * k + side],
                lsem.at[2 * k + side],
            )
            load.start()
            loads.append(load)
    mom_load = pltpu.make_async_copy(momentum_ref, mom_ref, csem.at[2])
    mom_load.start()
    flags = [jnp.where(live_ref[i] > 0, 1, 0) for i in range(n)]
    count = sum(flags)
    slot, before = [], 0
    for i in range(n):
        slot.append(jnp.where(flags[i] > 0, before, count + i - before))
        before = before + flags[i]
    order = [sum(jnp.where(slot[i] == s, i, 0) for i in range(n)) for s in range(slots)]
    slot = [jnp.minimum(place, slots - 1) for place in slot]
    barrier = pltpu.get_barrier_semaphore()
    for k in range(1, group):
        pl.semaphore_signal(barrier, inc=1, device_id=peer_id(k), device_id_type=MESH)
    for k in range(1, owners):
        pl.semaphore_signal(barrier, inc=1, device_id={"dp": owner_index(k)}, device_id_type=MESH)
    pl.semaphore_wait(barrier, group + owners - 2)

    psends = []
    for k in range(len(hops)):
        loads[2 * k].wait()
        for s in range(slots):
            pbuf[k, s] = gbuf[2 * k + 1][order[s]].astype(jnp.bfloat16)
        copy = pltpu.make_async_remote_copy(
            src_ref=pbuf.at[k], dst_ref=prbuf.at[k],
            send_sem=pssem.at[k], recv_sem=prsem.at[k],
            device_id={"grp": me_x * 2 + 1 - core}, device_id_type=MESH,
        )
        copy.start()
        psends.append(copy)
    sends = []
    for k, hop in enumerate(hops[:-1]):
        loads[2 * k + 1].wait()
        psends[k].wait_recv()
        for s in range(slots):
            pair = gbuf[2 * k][order[s]] + prbuf[k, s].astype(jnp.float32)
            sbuf[k, s] = pair.astype(jnp.bfloat16)
        copy = pltpu.make_async_remote_copy(
            src_ref=sbuf.at[k], dst_ref=rbuf.at[k],
            send_sem=ssem.at[k], recv_sem=rsem.at[k],
            device_id=chip_id(hop, core), device_id_type=MESH,
        )
        copy.start()
        sends.append(copy)
    last = len(hops) - 1
    loads[2 * last + 1].wait()
    psends[last].wait_recv()
    mom_load.wait()
    for s in range(slots):
        held = gbuf[2 * last][order[s]] + prbuf[last, s].astype(jnp.float32)
        fresh[s] = held + decay_rate * mom_ref[order[s]]
    for s in range(slots, owners * per):
        zsend[s] = jnp.zeros((rows, width), jnp.bfloat16)
    for copy in sends:
        copy.wait_recv()
    for s in range(slots):
        total = fresh[s]
        for k in range(last):
            total = total + rbuf[k, s].astype(jnp.float32)
        fresh[s] = total
        zsend[s] = total.astype(jnp.bfloat16)

    my_rows = pl.ds(pl.multiple_of(me_d * rows, rows), rows)
    own = pltpu.make_async_copy(
        zsend.at[pl.ds(me_d * per, per)], xbuf.at[:, my_rows, :], csem.at[0]
    )
    own.start()
    zcopies = []
    for k in range(1, owners):
        copy = pltpu.make_async_remote_copy(
            src_ref=zsend.at[pl.ds(owner_index(k) * per, per)], dst_ref=xbuf.at[:, my_rows, :],
            send_sem=zssem.at[k - 1], recv_sem=zrsem.at[k - 1],
            device_id={"dp": owner_index(k)}, device_id_type=MESH,
        )
        copy.start()
        zcopies.append(copy)
    alive = [jnp.full((1, width), flag, jnp.int32) > 0 for flag in flags]
    for i in range(n):
        new_ref[i] = jnp.where(alive[i], fresh[slot[i]], mom_ref[i])
    new_store = pltpu.make_async_copy(new_ref, new_hbm, csem.at[3])
    new_store.start()
    own.wait()
    for copy in zcopies:
        copy.wait_recv()

    for m in range(per):
        block = xbuf[m]
        gram = lax.dot_general(
            block, block, (((1,), (1,)), ((), ())), preferred_element_type=jnp.float32
        )
        gsend[m * full : (m + 1) * full] = gram.astype(jnp.bfloat16)
    my_half = pl.ds(pl.multiple_of(core * half, half), half)
    their_half = pl.ds(pl.multiple_of((1 - core) * half, half), half)
    partner = {"grp": me_x * 2 + 1 - core}
    to_pair = pltpu.make_async_remote_copy(
        src_ref=gsend.at[their_half], dst_ref=gpair,
        send_sem=hsem.at[0], recv_sem=hsem.at[1], device_id=partner, device_id_type=MESH,
    )
    to_pair.start()
    to_pair.wait_recv()
    total = gsend[my_half].astype(jnp.float32) + gpair[...].astype(jnp.float32)
    ghalf[...] = total.astype(jnp.bfloat16)
    gcopies = []
    for k, hop in enumerate(hops[:-1]):
        copy = pltpu.make_async_remote_copy(
            src_ref=ghalf, dst_ref=gchip.at[k],
            send_sem=gssem.at[k], recv_sem=grsem.at[k],
            device_id=chip_id(hop, core), device_id_type=MESH,
        )
        copy.start()
        gcopies.append(copy)
    for copy in gcopies:
        copy.wait_recv()
    for k in range(last):
        total = total + gchip[k].astype(jnp.float32)
    scale = math.sqrt(width * group)
    if per == 2:
        total = orthogonalizers([total])[0] * scale
    gsum[...] = total.astype(jnp.bfloat16)
    to_both = pltpu.make_async_remote_copy(
        src_ref=gsum, dst_ref=gfull.at[my_half],
        send_sem=hsem.at[2], recv_sem=hsem.at[3], device_id=partner, device_id_type=MESH,
    )
    to_both.start()
    gfull[my_half] = gsum[...]
    to_both.wait_recv()

    if per == 2:
        factors = [gfull[m * full : (m + 1) * full] for m in range(per)]
    else:
        factors = [orthogonalizers([gfull[...].astype(jnp.float32)])[0] * scale]
    for m in range(per):
        osend[m] = f32_dot(factors[m], xbuf[m]).astype(jnp.bfloat16)
    own = pltpu.make_async_copy(
        osend.at[:, my_rows, :], orecv.at[pl.ds(me_d * per, per)], csem.at[1]
    )
    own.start()
    ocopies = []
    for k in range(1, owners):
        their_rows = pl.ds(pl.multiple_of(owner_index(k) * rows, rows), rows)
        copy = pltpu.make_async_remote_copy(
            src_ref=osend.at[:, their_rows, :], dst_ref=orecv.at[pl.ds(me_d * per, per)],
            send_sem=ossem.at[k - 1], recv_sem=orsem.at[k - 1],
            device_id={"dp": owner_index(k)}, device_id_type=MESH,
        )
        copy.start()
        ocopies.append(copy)
    for copies in (psends, sends, zcopies, gcopies, [to_pair, to_both]):
        for copy in copies:
            copy.wait_send()
    own.wait()
    for copy in ocopies:
        copy.wait_recv()
    for i in range(n):
        part = orecv[slot[i]]
        orth_ref[i] = jnp.where(alive[i], part.astype(jnp.float32), 0.0).astype(jnp.bfloat16)
    for copy in ocopies:
        copy.wait_send()
    new_store.wait()


def fused_step(mesh, slots, number, grad_parts, momentum, live):
    n, rows, width = momentum.shape
    owners, per_group = mesh.shape["dp"], mesh.shape["grp"]
    group = mesh.shape["rep"] * per_group
    chips = group // 2
    per = -(-slots // owners)
    full = owners * rows
    half = per * full // 2
    bf16, f32 = jnp.bfloat16, jnp.float32
    dma = pltpu.SemaphoreType.DMA
    vmem = pl.BlockSpec(memory_space=pltpu.VMEM)
    smem = pl.BlockSpec(memory_space=pltpu.SMEM)
    hbm = pl.BlockSpec(memory_space=pl.ANY)
    return pl.pallas_call(
        functools.partial(step_kernel, (group, owners, per_group, n, rows, width, slots)),
        out_shape=(
            jax.ShapeDtypeStruct((n, rows, width), f32),
            jax.ShapeDtypeStruct((n, rows, width), bf16),
        ),
        in_specs=[hbm, hbm, smem],
        out_specs=(hbm, vmem),
        scratch_shapes=[
            pltpu.VMEM((n, rows, width), f32),
            pltpu.VMEM((n, rows, width), f32),
            pltpu.VMEM((chips, slots, rows, width), bf16),
            pltpu.VMEM((chips, slots, rows, width), bf16),
            pltpu.VMEM((chips - 1, slots, rows, width), bf16),
            pltpu.VMEM((chips - 1, slots, rows, width), bf16),
            pltpu.VMEM((slots, rows, width), f32),
            pltpu.VMEM((owners * per, rows, width), bf16),
            pltpu.VMEM((per, full, width), bf16),
            pltpu.VMEM((per * full, full), bf16),
            pltpu.VMEM((half, full), bf16),
            pltpu.VMEM((half, full), bf16),
            pltpu.VMEM((chips - 1, half, full), bf16),
            pltpu.VMEM((half, full), bf16),
            pltpu.VMEM((per * full, full), bf16),
            pltpu.VMEM((per, full, width), bf16),
            pltpu.VMEM((owners * per, rows, width), bf16),
            dma((group,)),
            dma((chips,)),
            dma((chips,)),
            dma((chips - 1,)),
            dma((chips - 1,)),
            dma((owners - 1,)),
            dma((owners - 1,)),
            dma((chips - 1,)),
            dma((chips - 1,)),
            dma((4,)),
            dma((owners - 1,)),
            dma((owners - 1,)),
            dma((4,)),
            *[pltpu.VMEM((n, rows, width), f32) for _ in range(group)],
        ],
        compiler_params=pltpu.CompilerParams(
            collective_id=number, has_side_effects=True, vmem_limit_bytes=48 * 1024 * 1024
        ),
    )(grad_parts, momentum, live)


def per_device_step(mesh, grad_parts, momentum, layer_live):
    n, rows, width = momentum.shape
    owners, per_group = mesh.shape["dp"], mesh.shape["grp"]
    group = mesh.shape["rep"] * per_group
    fits = (
        width % 128 == 0
        and rows % 16 == 0
        and (owners * rows) % 32 == 0
        and n * rows * width * group * 12 < 40 * 1024 * 1024
        and per_group % 2 == 0
        and 2 < n <= 2 * owners
        and group > 2
        and owners > 1
    )
    if not fits:
        return per_device(grad_parts, momentum, layer_live)
    sizes = range(2, n + 1)
    index = jnp.sum((layer_live > 0).astype(jnp.int32)) - sizes[0]
    branches = [
        functools.partial(fused_step, mesh, size, number) for number, size in enumerate(sizes)
    ]
    return lax.switch(index, branches, grad_parts, momentum, layer_live)


def solution(mesh):
    placed = (P(("rep", "grp"), None, "dp", None), P(None, "dp", ("rep", "grp")), P())
    return jax.shard_map(
        functools.partial(per_device_step, mesh),
        mesh=mesh,
        in_specs=placed,
        out_specs=(P(None, "dp", ("rep", "grp")), P(None, "dp", ("rep", "grp"))),
        check_vma=False,
    )
```
